32 devices in a mesh: seq: 8 (over z, y), mp: 2 (over x), dp: 2 (over core).
Axes of the slice: x: 2, y: 2, z: 4, core: 2. Of those that a mesh axis runs over, the one named last changes fastest.
Arguments:
- encoder_hidden: bfloat16 [2, 896, 4096], P('dp', 'seq'), may hold values from -6 to 6
- kv_weight: bfloat16 [4096, 2, 2048], P(None, None, 'mp')
- self_proj: bfloat16 [2, 512, 3, 2048], P('dp', 'seq', None, 'mp'), may hold values from -20 to 20
- cross_query: bfloat16 [2, 512, 2048], P('dp', 'seq', 'mp'), may hold values from -12 to 12
- cotangents: bfloat16 [2, 512, 2, 2048], P('dp', 'seq', None, 'mp'), may hold values from -6 to 6
- position_bias: float32 [8, 8], replicated, may hold values from -4 to 4
- input_lengths: int32 [2, 8, 8], P('dp', 'seq'), may hold values from 1 to 32, 112 in all within a row
- target_home: int32 [2, 8, 8], P('dp', 'seq'), may hold values from 0 to 7, each once within a row
- target_lengths: int32 [2, 8, 8], P('dp', 'seq'), may hold values from 1 to 8, 40 in all within a row
- drop_seed: int32 [1], replicated, may hold values from 0 to 999999
Outputs:
- cross_output: bfloat16 [2, 512, 2048], P('dp', 'seq', 'mp')
- self_output: bfloat16 [2, 512, 2048], P('dp', 'seq', 'mp')
- decoder_grads: bfloat16 [2, 512, 4, 2048], P('dp', 'seq', None, 'mp')
- hidden_grads: bfloat16 [2, 896, 4096], P('dp', 'seq', 'mp')
- position_grad: float32 [8, 8], replicated
The draws below stay inside these ranges and needn't reach their ends.
Inputs may be any that keep to these rules, and one draw needn't show every extreme that they name: `input_lengths`: each encoder shard sends exactly one example to each decoder shard; the input lengths of one shard fill its 112 rows, and some example has exactly 32. `target_home`: per encoder shard, each decoder shard is named once. `target_lengths`: the target lengths of one decoder shard sum to 40, and some slot has exactly 8.
All inputs are finite; a program needn't handle non-finite values.
Results may differ from the reference program's by a relative error of at most 0.004.
The reference program's roundings to bfloat16 on the way count: a program that leaves them out, or rounds other values in their place, can miss the bound.
Values may be sent and summed in bfloat16 or wider, within the bound.
A program may use at most 64 MiB of HBM per device.

```python
import math
import jax
import jax.numpy as jnp
import numpy as np
from jax import lax

D_MODEL = 4096
HEADS = 8
HEAD = 256
IN_MAX = 32
TGT_MAX = 8
ENC_DEV = 112
DEC_DEV = 64
ENC_ROWS = 896
DEC_ROWS = 512
GROUPS = 2
FEATURES = 2048
N_SEQ = 8
N_MP = 2


def draw_encoder_hidden(key, part):
    shape = (GROUPS, ENC_ROWS, D_MODEL)
    return jnp.clip(jax.random.normal(jax.random.fold_in(key, 21), shape, jnp.float32), -6.0, 6.0).astype(jnp.bfloat16)


def draw_kv_weight(key, part):
    shape = (D_MODEL, 2, FEATURES)
    spread = D_MODEL ** (-0.5)
    return (jnp.clip(jax.random.normal(jax.random.fold_in(key, 31), shape, jnp.float32), -6.0, 6.0) * spread).astype(jnp.bfloat16)


def draw_cross_query(key, part):
    shape = (GROUPS, DEC_ROWS, FEATURES)
    return jnp.clip(jax.random.normal(jax.random.fold_in(key, 11), shape, jnp.float32), -6.0, 6.0).astype(jnp.bfloat16)


def draw_self_proj(key, part):
    shape = (GROUPS, DEC_ROWS, 3, FEATURES)
    return jnp.clip(jax.random.normal(jax.random.fold_in(key, 41), shape, jnp.float32), -6.0, 6.0).astype(jnp.bfloat16)


def block_scale(stream_key, shape, split, smallest, largest):
    factor_of, own = 1.0, jax.random.fold_in(stream_key, 6)
    for dim, blocks in split:
        heights = jnp.exp(jax.random.uniform(jax.random.fold_in(own, dim), (blocks,), jnp.float32, smallest / len(split), largest / len(split)))
        factor_of = factor_of * jnp.repeat(heights, shape[dim] // blocks).reshape([-1 if axis == dim else 1 for axis in range(len(shape))])
    return factor_of


def split_up(count, total, limit, lean):
    loads = [(1 << 20) // math.isqrt(grade ** lean) + 1 for grade in range(2, count + 1)]
    spare, given = total - limit - (count - 1), [1] * (count - 1)
    while spare > 0:
        movable = [i for i in range(count - 1) if given[i] < limit]
        whole, budget = sum([loads[i] for i in movable]), spare
        for i in movable:
            extra = min(limit - given[i], max(1, budget * loads[i] // whole), spare)
            given[i] = given[i] + extra
            spare = spare - extra
    return np.array([limit] + given)


def uneven_parts(key, amount, total, limit, skew):
    if amount == 2:
        one = jax.random.randint(key, (), max(1, total - limit), min(limit, total - 1) + 1)
        return jnp.stack([one, total - one])
    sizes = jnp.asarray(split_up(amount, total, limit, skew), jnp.int32)
    couples = (amount - 1) // 2
    donor, sink = sizes[1:1 + 2 * couples:2], sizes[2:2 + 2 * couples:2]
    margin = jnp.minimum(donor - 1, limit - sink)
    shifted = jax.random.randint(jax.random.fold_in(key, 1), (couples,), 0, 1 << 20) % (margin + 1)
    sizes = sizes.at[1:1 + 2 * couples:2].set(donor - shifted).at[2:2 + 2 * couples:2].set(sink + shifted)
    return sizes[jax.random.permutation(jax.random.fold_in(key, 2), amount)]


def centred(own_key, dims, scale, limit, shards=(), held_as=jnp.bfloat16):
    values = jax.random.normal(own_key, dims, jnp.float32) * scale
    if len(shards) > 0:
        values = block_scale(own_key, dims, shards, -0.22, 0.18) * values
    return jnp.clip(values, min=-limit, max=limit).astype(held_as)


def setup_inputs(seed: int = 0) -> dict:
    streams_of = jax.random.split(jax.random.key(seed), 11)
    return {
        "encoder_hidden": draw_encoder_hidden(jax.random.fold_in(streams_of[10], 71), 0),
        "kv_weight": draw_kv_weight(jax.random.fold_in(streams_of[10], 71), 0),
        "self_proj": draw_self_proj(jax.random.fold_in(streams_of[10], 71), 0),
        "cross_query": draw_cross_query(jax.random.fold_in(streams_of[10], 71), 0),
        "cotangents": centred(streams_of[4], (GROUPS, DEC_ROWS, 2, FEATURES), 1.0, 6.0, ((0, 2), (1, 8), (3, 2))),
        "position_bias": centred(streams_of[5], (TGT_MAX, HEADS), 1.0, 4.0, (), jnp.float32),
        "input_lengths": jax.vmap(lambda own: uneven_parts(own, N_SEQ, ENC_DEV, IN_MAX, 2))(jax.random.split(streams_of[6], GROUPS * N_SEQ)).reshape((GROUPS, N_SEQ, N_SEQ)).astype(jnp.int32),
        "target_home": jax.vmap(lambda own: jax.random.permutation(own, N_SEQ))(jax.random.split(streams_of[7], GROUPS * N_SEQ)).reshape((GROUPS, N_SEQ, N_SEQ)).astype(jnp.int32),
        "target_lengths": jax.vmap(lambda own: uneven_parts(own, N_SEQ, DEC_DEV * 5 // 8, TGT_MAX, 2))(jax.random.split(streams_of[8], GROUPS * N_SEQ)).reshape((GROUPS, N_SEQ, N_SEQ)).astype(jnp.int32),
        "drop_seed": jax.random.randint(streams_of[9], (1,), 0, 1000000).astype(jnp.int32),
    }


drop_limit = 6554
keep_factor = 65536.0 / (65536.0 - 6554.0)


def scramble(state):
    state = state ^ ((state >> 16) & 65535)
    state = state * 73244475
    state = state ^ ((state >> 16) & 65535)
    state = state * 73244475
    state = state ^ ((state >> 16) & 65535)
    return state


def keep_table(drop_value, tag, batch_group, head_ids, query_pos, key_pos):
    state = scramble(drop_value + tag * 7919 + batch_group * 104729)
    state = scramble(state + head_ids[None, :, None, None])
    state = scramble(state + query_pos[:, None, :, None])
    state = scramble(state + key_pos[:, None, None, :])
    return jnp.where((state & 65535) >= drop_limit, keep_factor, 0.0).astype(jnp.float32)


def attend(queries, keys_in, values_in, grad_out, query_pos, key_pos, query_count, key_count, head_ids, tag, drop_value, batch_group, bias_table, causal):
    width = queries.shape[3]
    factor = width ** -0.5
    query_index = jnp.arange(queries.shape[1], dtype=jnp.int32)
    key_index = jnp.arange(keys_in.shape[1], dtype=jnp.int32)
    scores = jnp.einsum("bqhe,bkhe->bhqk", queries.astype(jnp.float32), keys_in.astype(jnp.float32)) * factor
    allowed = (key_index[None, :] < key_count[:, None])[:, None, None, :]
    onehot = None
    if causal:
        distance = query_index[:, None] - key_index[None, :]
        allowed = allowed & (distance >= 0)[None, None]
        onehot = (distance[:, :, None] == jnp.arange(bias_table.shape[0], dtype=jnp.int32)[None, None, :]).astype(jnp.float32)
        scores = scores + jnp.einsum("qkr,rh->hqk", onehot, bias_table, precision=lax.Precision.HIGHEST)[None]
    scores = jnp.where(allowed, scores, -1e30)
    peak = jnp.max(scores, axis=-1, keepdims=True)
    expo = jnp.exp(scores - peak)
    probs = expo / jnp.sum(expo, axis=-1, keepdims=True)
    live = (query_index[None, :] < query_count[:, None])[:, None, :, None]
    keep = keep_table(drop_value, tag, batch_group, head_ids, query_pos, key_pos)
    weights = jnp.where(live, probs * keep, 0.0).astype(jnp.bfloat16)
    attended = jnp.einsum("bhqk,bkhe->bqhe", weights.astype(jnp.float32), values_in.astype(jnp.float32)).astype(jnp.bfloat16)
    dweights = jnp.einsum("bqhe,bkhe->bhqk", grad_out.astype(jnp.float32), values_in.astype(jnp.float32))
    dprobs = dweights * keep
    delta = jnp.sum(probs * dprobs, axis=-1, keepdims=True)
    dscores = jnp.where(live, probs * (dprobs - delta), 0.0)
    scaled = (dscores * factor).astype(jnp.bfloat16)
    query_grad = jnp.einsum("bhqk,bkhe->bqhe", scaled.astype(jnp.float32), keys_in.astype(jnp.float32)).astype(jnp.bfloat16)
    key_grad = jnp.einsum("bhqk,bqhe->bkhe", scaled.astype(jnp.float32), queries.astype(jnp.float32)).astype(jnp.bfloat16)
    value_grad = jnp.einsum("bhqk,bqhe->bkhe", weights.astype(jnp.float32), grad_out.astype(jnp.float32)).astype(jnp.bfloat16)
    bias_grad = None
    if causal:
        bias_grad = jnp.einsum("bhqk,qkr->rh", dscores, onehot, precision=lax.Precision.HIGHEST)
    return attended, query_grad, key_grad, value_grad, bias_grad


def reference(encoder_hidden, kv_weight, self_proj, cross_query, cotangents, position_bias, input_lengths, target_home, target_lengths, drop_seed):
    head_ids = jnp.arange(HEADS, dtype=jnp.int32)
    drop_value = drop_seed[0]
    flat_weight = kv_weight.reshape(D_MODEL, 2 * FEATURES)
    block_width = FEATURES // N_MP

    def one_group(batch_group):
        hidden_rows = encoder_hidden[batch_group]
        kv_rows = jnp.dot(hidden_rows, flat_weight, preferred_element_type=jnp.float32).astype(jnp.bfloat16).reshape(ENC_ROWS, 2, FEATURES)
        padded = jnp.concatenate([kv_rows, jnp.zeros((IN_MAX, 2, FEATURES), jnp.bfloat16)], axis=0)
        lengths = input_lengths[batch_group]
        homes = target_home[batch_group]
        offsets = (jnp.cumsum(lengths, axis=1) - lengths).astype(jnp.int32)
        matched = (homes[:, None, :] == jnp.arange(N_SEQ, dtype=jnp.int32)[None, :, None]).astype(jnp.int32)
        piece_off = jnp.sum(matched * offsets[:, None, :], axis=2).astype(jnp.int32)
        piece_len = jnp.sum(matched * lengths[:, None, :], axis=2).astype(jnp.int32)
        starts = (jnp.arange(N_SEQ, dtype=jnp.int32)[:, None] * ENC_DEV + piece_off).astype(jnp.int32)

        def one_device(target):
            first = starts[:, target]
            blocks = jax.vmap(lambda row_begin: lax.dynamic_slice_in_dim(padded, row_begin, IN_MAX, 0))(first)
            key_rows = blocks[:, :, 0].reshape(N_SEQ, IN_MAX, HEADS, HEAD)
            value_rows = blocks[:, :, 1].reshape(N_SEQ, IN_MAX, HEADS, HEAD)
            row_start = (target * DEC_DEV).astype(jnp.int32)
            queries = lax.dynamic_slice_in_dim(cross_query[batch_group], row_start, DEC_DEV, 0).reshape(N_SEQ, TGT_MAX, HEADS, HEAD)
            grads_in = lax.dynamic_slice_in_dim(cotangents[batch_group], row_start, DEC_DEV, 0)
            self_rows = lax.dynamic_slice_in_dim(self_proj[batch_group], row_start, DEC_DEV, 0)
            query_pos = (row_start + jnp.arange(DEC_DEV, dtype=jnp.int32)).reshape(N_SEQ, TGT_MAX)
            key_pos = (first[:, None] + jnp.arange(IN_MAX, dtype=jnp.int32)[None, :]).astype(jnp.int32)
            counts = target_lengths[batch_group, target]
            cross = attend(queries, key_rows, value_rows, grads_in[:, 1].reshape(N_SEQ, TGT_MAX, HEADS, HEAD), query_pos, key_pos, counts, piece_len[:, target], head_ids, 0, drop_value, batch_group, position_bias, False)
            own = attend(self_rows[:, 0].reshape(N_SEQ, TGT_MAX, HEADS, HEAD), self_rows[:, 1].reshape(N_SEQ, TGT_MAX, HEADS, HEAD), self_rows[:, 2].reshape(N_SEQ, TGT_MAX, HEADS, HEAD), grads_in[:, 0].reshape(N_SEQ, TGT_MAX, HEADS, HEAD), query_pos, query_pos, counts, counts, head_ids, 1, drop_value, batch_group, position_bias, True)
            return cross[0], cross[1], cross[2], cross[3], own[0], own[1], own[2], own[3], own[4]

        results = lax.map(one_device, jnp.arange(N_SEQ, dtype=jnp.int32))
        cross_out, cross_dq, cross_dk, cross_dv, self_out, self_dq, self_dk, self_dv, bias_part = results
        cross_output = cross_out.reshape(DEC_ROWS, FEATURES)
        self_output = self_out.reshape(DEC_ROWS, FEATURES)
        decoder_grads = jnp.stack([self_dq.reshape(DEC_ROWS, FEATURES), self_dk.reshape(DEC_ROWS, FEATURES), self_dv.reshape(DEC_ROWS, FEATURES), cross_dq.reshape(DEC_ROWS, FEATURES)], axis=1)
        key_index = (starts.T[:, :, None] + jnp.arange(IN_MAX, dtype=jnp.int32)[None, None, :]).astype(jnp.int32)
        key_grads = jnp.stack([cross_dk.reshape(N_SEQ, N_SEQ, IN_MAX, FEATURES), cross_dv.reshape(N_SEQ, N_SEQ, IN_MAX, FEATURES)], axis=3)
        total = jnp.zeros((ENC_ROWS + IN_MAX, 2, FEATURES), jnp.float32).at[key_index].add(key_grads.astype(jnp.float32))
        kv_grads = total[:ENC_ROWS].astype(jnp.bfloat16)
        hidden_grad = jnp.zeros((ENC_ROWS, D_MODEL), jnp.float32)
        for column_block in range(N_MP):
            grad_block = kv_grads[:, :, column_block * block_width:(column_block + 1) * block_width].reshape(ENC_ROWS, 2 * block_width)
            weight_block = kv_weight[:, :, column_block * block_width:(column_block + 1) * block_width].reshape(D_MODEL, 2 * block_width)
            partial_term = jnp.dot(grad_block, weight_block.T, preferred_element_type=jnp.float32).astype(jnp.bfloat16)
            partial_term = lax.optimization_barrier(partial_term)
            hidden_grad = hidden_grad + partial_term.astype(jnp.float32)
        return cross_output, self_output, decoder_grads, hidden_grad.astype(jnp.bfloat16), jnp.sum(bias_part, axis=0)

    cross_output, self_output, decoder_grads, hidden_grads, bias_parts = lax.map(one_group, jnp.arange(GROUPS, dtype=jnp.int32))
    return cross_output, self_output, decoder_grads, hidden_grads, jnp.sum(bias_parts, axis=0)
```

```python
import functools

import jax
import jax.numpy as jnp
from jax import lax
from jax.experimental import pallas as pl
from jax.experimental.pallas import tpu as pltpu
from jax.sharding import PartitionSpec as P

HEAD = 256
TGT_MAX = 8
PIECES = 8
STAGE = 256
EARLY = 7

MESH = pl.DeviceIdType.MESH
drop_limit = 6554
keep_factor = 65536.0 / (65536.0 - 6554.0)


def scramble(state):
    state = state ^ ((state >> 16) & 65535)
    state = state * 73244475
    state = state ^ ((state >> 16) & 65535)
    state = state * 73244475
    state = state ^ ((state >> 16) & 65535)
    return state


def keep_table(base, head, query_pos, key_pos):
    state = scramble(base + head)
    state = scramble(state + query_pos)
    state = scramble(state + key_pos)
    return jnp.where((state & 65535) >= drop_limit, keep_factor, 0.0).astype(jnp.float32)


def nt(a, b):
    return lax.dot_general(a, b, (((1,), (1,)), ((), ())), preferred_element_type=jnp.float32)


def nn(a, b):
    return lax.dot_general(a, b, (((1,), (0,)), ((), ())), preferred_element_type=jnp.float32)


def tn(a, b):
    return lax.dot_general(a, b, (((0,), (0,)), ((), ())), preferred_element_type=jnp.float32)


def softmax(scores):
    peak = jnp.max(scores, axis=-1, keepdims=True)
    expo = jnp.exp(scores - peak)
    return expo / jnp.sum(expo, axis=-1, keepdims=True)


def kernel(
    sizes,
    lengths_in,
    homes_in,
    counts_in,
    seed_in,
    bias_in,
    hidden_in,
    weight,
    self_in,
    query_in,
    cotangents_in,
    self_out,
    cross_out,
    decoder_grads,
    hidden_out,
    position_out,
    lengths,
    homes,
    counts,
    seed,
    bias,
    hidden,
    self_proj,
    cross_query,
    cotangents,
    stage,
    w_buf,
    kv_acc,
    kv_buf,
    grad_buf,
    self_grad,
    planes,
    sent,
    got,
    reply,
    got_reply,
    partial_send,
    partial_got,
    pos_seq,
    pos_all,
    w_sem,
    x_send,
    x_recv,
    r_send,
    r_recv,
    h_send,
    h_recv,
    p_send,
    p_recv,
    a_send,
    a_recv,
    in_sem,
):
    seq, mp, dp = sizes
    me = lax.axis_index("seq")
    column = lax.axis_index("mp")
    group = lax.axis_index("dp")
    enc = hidden.shape[0]
    model = hidden.shape[1]
    dec, features = cross_query.shape
    heads = features // HEAD
    factor = HEAD ** (-0.5)
    rows2 = 2 * TGT_MAX
    others = mp * dp
    mine = column * dp + group
    steps = model // STAGE

    def w_copy(n):
        return pltpu.make_async_copy(
            weight.at[pl.ds(n * STAGE, STAGE)], stage.at[n], w_sem.at[n]
        )

    def other_id(k):
        other = lax.rem(mine + k, others)
        return {"mp": other // dp, "dp": lax.rem(other, dp)}

    barrier = pltpu.get_barrier_semaphore()
    for k in range(1, seq):
        pl.semaphore_signal(
            barrier, inc=1, device_id={"seq": lax.rem(me + k, seq)}, device_id_type=MESH
        )

    def greet(k, carry):
        pl.semaphore_signal(barrier, inc=1, device_id=other_id(k), device_id_type=MESH)
        return carry

    lax.fori_loop(1, others, greet, 0)
    incoming = [
        pltpu.make_async_copy(source, target, in_sem.at[i])
        for i, (source, target) in enumerate(
            (
                (counts_in, counts),
                (query_in, cross_query),
                (cotangents_in, cotangents),
                (seed_in, seed),
                (bias_in, bias),
                (self_in, self_proj),
                (hidden_in, hidden),
                (lengths_in, lengths),
                (homes_in, homes),
            )
        )
    ]
    for copy in incoming:
        copy.start()

    def load(n, carry):
        w_copy(n).start()
        return carry

    lax.fori_loop(0, steps, load, 0)
    for copy in incoming[:3]:
        copy.wait()

    def pick(value, which):
        return value.reshape(seq, 2, TGT_MAX, value.shape[1])[:, which].reshape(
            dec, value.shape[1]
        )

    def mix(first, second):
        shape = (seq, 1, TGT_MAX, first.shape[1])
        return jnp.concatenate([first.reshape(shape), second.reshape(shape)], axis=1).reshape(
            2 * dec, first.shape[1]
        )

    def live_rows(width):
        row = lax.broadcasted_iota(jnp.int32, (dec, width), 0)
        count = jnp.zeros((dec, width), jnp.int32)
        for s in range(seq):
            count = jnp.where((row >> 3) == s, counts[s], count)
        return (row & 7) < count

    both_grads = jnp.swapaxes(cotangents[...], 0, 1)
    self_grad[...] = both_grads[0]
    cross_grad = jnp.where(live_rows(features), both_grads[1].astype(jnp.float32), 0.0)
    sent[...] = mix(cross_query[...].astype(jnp.float32), cross_grad).astype(jnp.bfloat16)

    def slot(ref, index):
        return ref.at[pl.ds(pl.multiple_of(index * rows2, rows2), rows2), :]

    def x_copy(k):
        to = lax.rem(me + k, seq)
        return pltpu.make_async_remote_copy(
            src_ref=slot(sent, to),
            dst_ref=slot(got, me),
            send_sem=x_send.at[k],
            recv_sem=x_recv.at[k],
            device_id={"seq": to},
            device_id_type=MESH,
        )

    def r_copy(k):
        to = lax.rem(me + k, seq)
        return pltpu.make_async_remote_copy(
            src_ref=slot(reply, to),
            dst_ref=slot(got_reply, me),
            send_sem=r_send.at[k],
            recv_sem=r_recv.at[k],
            device_id={"seq": to},
            device_id_type=MESH,
        )

    def p_copy(k):
        return pltpu.make_async_remote_copy(
            src_ref=pos_seq.at[me],
            dst_ref=pos_seq.at[me],
            send_sem=p_send.at[k],
            recv_sem=p_recv.at[k],
            device_id={"seq": lax.rem(me + k, seq)},
            device_id_type=MESH,
        )

    def a_copy(k):
        return pltpu.make_async_remote_copy(
            src_ref=pos_all.at[mine],
            dst_ref=pos_all.at[mine],
            send_sem=a_send.at[k],
            recv_sem=a_recv.at[k],
            device_id=other_id(k),
            device_id_type=MESH,
        )

    own_rows = pl.ds(pl.multiple_of(me * rows2, rows2), rows2)
    got[own_rows, :] = sent[own_rows, :]
    for copy in incoming[3:6]:
        copy.wait()

    row = lax.broadcasted_iota(jnp.int32, (dec, dec), 0)
    col = lax.broadcasted_iota(jnp.int32, (dec, dec), 1)
    count = jnp.zeros((dec, dec), jnp.int32)
    for s in range(seq):
        count = jnp.where((row >> 3) == s, counts[s], count)
    distance = row - col
    allowed = ((row >> 3) == (col >> 3)) & (distance >= 0) & ((col & 7) < count)
    live = (row & 7) < count
    base = scramble(seed[0] + 7919 + group * 104729)
    lane = lax.broadcasted_iota(jnp.int32, (TGT_MAX, 128), 1)
    position = jnp.zeros((TGT_MAX, 128), jnp.float32)
    for h in range(heads):
        cols = slice(h * HEAD, (h + 1) * HEAD)
        head = column * heads + h
        q, key, val = self_proj[0, :, cols], self_proj[1, :, cols], self_proj[2, :, cols]
        grad = self_grad[:, cols]
        shift = jnp.zeros((dec, dec), jnp.float32)
        for r in range(TGT_MAX):
            shift = jnp.where(distance == r, bias[r, head], shift)
        probs = softmax(jnp.where(allowed, nt(q, key) * factor + shift, -1e30))
        keep = keep_table(base, head, me * dec + row, me * dec + col)
        weights = jnp.where(live, probs * keep, 0.0).astype(jnp.bfloat16)
        self_out[:, cols] = nn(weights, val).astype(jnp.bfloat16)
        dprobs = nt(grad, val) * keep
        delta = jnp.sum(probs * dprobs, axis=-1, keepdims=True)
        dscores = jnp.where(live, probs * (dprobs - delta), 0.0)
        scaled = (dscores * factor).astype(jnp.bfloat16)
        planes[0, :, cols] = nn(scaled, key).astype(jnp.bfloat16)
        planes[1, :, cols] = tn(scaled, q).astype(jnp.bfloat16)
        planes[2, :, cols] = tn(weights, grad).astype(jnp.bfloat16)
        sums = jnp.concatenate(
            [
                jnp.sum(jnp.where(distance == r, dscores, 0.0), axis=0, keepdims=True)
                for r in range(TGT_MAX)
            ],
            axis=0,
        )
        total = jnp.sum(sums, axis=1, keepdims=True)
        position = jnp.where(lane == head, total, position)
    pos_seq[me] = position

    kv_acc[...] = jnp.zeros_like(kv_acc)
    for copy in incoming[6:]:
        copy.wait()

    def project(n, carry):
        w_copy(n).wait()
        rows = pl.ds(pl.multiple_of(n * STAGE, STAGE), STAGE)
        part = jnp.swapaxes(stage[n], 0, 1)
        w_buf[:, rows, :] = part
        left = hidden[:, rows]
        kv_acc[0] += nn(left, part[0])
        kv_acc[1] += nn(left, part[1])

        @pl.when(n == EARLY)
        def _():
            pl.semaphore_wait(barrier, seq - 1 + others - 1)
            for k in range(1, seq):
                x_copy(k).start()
            for k in range(1, seq):
                p_copy(k).start()

        return carry

    lax.fori_loop(0, steps, project, 0)
    kv_buf[...] = kv_acc[...].astype(jnp.bfloat16)

    for k in range(1, seq):
        x_copy(k).wait()

    row = lax.broadcasted_iota(jnp.int32, (dec, enc), 0)
    col = lax.broadcasted_iota(jnp.int32, (dec, enc), 1)
    home = jnp.zeros((dec, enc), jnp.int32)
    offset = jnp.int32(0)
    for e in range(seq):
        home = jnp.where(col >= offset, homes[e], home)
        offset = offset + lengths[e]
    allowed = (row >> 3) == home
    query_pos = (row >> 3) * dec + me * TGT_MAX + (row & 7)
    key_pos = me * enc + col
    base = scramble(seed[0] + group * 104729)
    blank = jnp.zeros((dec, enc), jnp.float32)
    for h in range(heads):
        cols = slice(h * HEAD, (h + 1) * HEAD)
        head = column * heads + h
        both = got[:, cols]
        key, val = kv_buf[0, :, cols], kv_buf[1, :, cols]
        probs = softmax(jnp.where(allowed, pick(nt(both, key), 0) * factor, -1e30))
        keep = keep_table(base, head, query_pos, key_pos)
        weights = probs * keep
        dprobs = pick(nt(both, val), 1) * keep
        delta = jnp.sum(probs * dprobs, axis=-1, keepdims=True)
        scaled = probs * (dprobs - delta) * factor
        grad_buf[0, :, cols] = tn(mix(scaled, blank).astype(jnp.bfloat16), both).astype(
            jnp.bfloat16
        )
        grad_buf[1, :, cols] = tn(mix(blank, weights).astype(jnp.bfloat16), both).astype(
            jnp.bfloat16
        )
        reply[:, cols] = mix(
            nn(weights.astype(jnp.bfloat16), val), nn(scaled.astype(jnp.bfloat16), key)
        ).astype(jnp.bfloat16)

    share = model // mp
    piece = share // PIECES

    def product(begin):
        rows = pl.ds(begin, piece)
        total = nt(grad_buf[0], w_buf[0, rows, :]) + nt(grad_buf[1], w_buf[1, rows, :])
        return total.astype(jnp.bfloat16)

    def h_copy(k, i):
        return pltpu.make_async_remote_copy(
            src_ref=partial_send.at[k, i],
            dst_ref=partial_got.at[column, i],
            send_sem=h_send.at[k, i],
            recv_sem=h_recv.at[k, i],
            device_id={"mp": lax.rem(column + k, mp)},
            device_id_type=MESH,
        )

    for k in range(1, seq):
        r_copy(k).start()
    for k in range(1, mp):
        to = lax.rem(column + k, mp)

        def send_piece(i, carry, k=k, to=to):
            partial_send[k, i] = product(pl.multiple_of(to * share + i * piece, piece))
            h_copy(k, i).start()
            return carry

        lax.fori_loop(0, PIECES, send_piece, 0)

    got_reply[own_rows, :] = reply[own_rows, :]
    for k in range(1, seq):
        p_copy(k).wait()
    total = pos_seq[0]
    for s in range(1, seq):
        total = total + pos_seq[s]
    pos_all[mine] = total

    def share_total(k, carry):
        a_copy(k).start()
        return carry

    lax.fori_loop(1, others, share_total, 0)

    def keep_piece(i, carry):
        partial_got[column, i] = product(pl.multiple_of(column * share + i * piece, piece))
        return carry

    lax.fori_loop(0, PIECES, keep_piece, 0)
    for k in range(1, seq):
        r_copy(k).wait()
    back = got_reply[...].astype(jnp.float32)
    cross_out[...] = jnp.where(live_rows(features), pick(back, 0), 0.0).astype(jnp.bfloat16)
    planes[3] = pick(back, 1).astype(jnp.bfloat16)
    decoder_grads[...] = jnp.swapaxes(planes[...], 0, 1)

    def take_total(k, carry):
        a_copy(k).wait()
        return carry

    lax.fori_loop(1, others, take_total, 0)
    total = pos_all[0]
    for m in range(1, others):
        total = total + pos_all[m]
    position_out[...] = total[:, : position_out.shape[1]]

    for i in range(PIECES):
        for k in range(1, mp):
            h_copy(k, i).wait()
        total = partial_got[0, i].astype(jnp.float32)
        for m in range(1, mp):
            total = total + partial_got[m, i].astype(jnp.float32)
        hidden_out[:, i * piece : (i + 1) * piece] = total.astype(jnp.bfloat16)


def deliver(*refs):
    taken, given, done = refs[:5], refs[5:10], refs[10]
    copies = [pltpu.make_async_copy(taken[i], given[i], done.at[i]) for i in range(5)]
    for copy in copies:
        copy.start()
    for copy in copies:
        copy.wait()


def body(
    sizes,
    encoder_hidden,
    kv_weight,
    self_proj,
    cross_query,
    cotangents,
    position_bias,
    input_lengths,
    target_home,
    target_lengths,
    drop_seed,
):
    seq, mp, dp = sizes
    enc, model = encoder_hidden.shape[1:]
    dec, features = cross_query.shape[1:]
    share = model // mp
    others = mp * dp
    vmem = pl.BlockSpec(memory_space=pltpu.VMEM)
    far = pl.BlockSpec(memory_space=pltpu.HBM)
    hbm = pl.BlockSpec(memory_space=pl.ANY)
    half = jnp.bfloat16
    dma = pltpu.SemaphoreType.DMA
    shapes = [
        jax.ShapeDtypeStruct((dec, features), half),
        jax.ShapeDtypeStruct((dec, features), half),
        jax.ShapeDtypeStruct((dec, 4, features), half),
        jax.ShapeDtypeStruct((enc, share), half),
        jax.ShapeDtypeStruct(position_bias.shape, jnp.float32),
    ]
    results = pl.pallas_call(
        functools.partial(kernel, sizes),
        out_shape=tuple(shapes),
        in_specs=[far] * 10,
        out_specs=(vmem,) * 5,
        scratch_shapes=[
            pltpu.SMEM((seq,), jnp.int32),
            pltpu.SMEM((seq,), jnp.int32),
            pltpu.SMEM((seq,), jnp.int32),
            pltpu.SMEM((1,), jnp.int32),
            pltpu.SMEM(position_bias.shape, jnp.float32),
            pltpu.VMEM((enc, model), half),
            pltpu.VMEM((3, dec, features), half),
            pltpu.VMEM((dec, features), half),
            pltpu.VMEM((dec, 2, features), half),
            pltpu.VMEM((model // STAGE, STAGE, 2, features), half),
            pltpu.VMEM((2, model, features), half),
            pltpu.VMEM((2, enc, features), jnp.float32),
            pltpu.VMEM((2, enc, features), half),
            pltpu.VMEM((2, enc, features), half),
            pltpu.VMEM((dec, features), half),
            pltpu.VMEM((4, dec, features), half),
            pltpu.VMEM((2 * dec, features), half),
            pltpu.VMEM((2 * dec, features), half),
            pltpu.VMEM((2 * dec, features), half),
            pltpu.VMEM((2 * dec, features), half),
            pltpu.VMEM((mp, PIECES, enc, share // PIECES), half),
            pltpu.VMEM((mp, PIECES, enc, share // PIECES), half),
            pltpu.VMEM((seq, TGT_MAX, 128), jnp.float32),
            pltpu.VMEM((others, TGT_MAX, 128), jnp.float32),
            dma((model // STAGE,)),
            dma((seq,)),
            dma((seq,)),
            dma((seq,)),
            dma((seq,)),
            dma((mp, PIECES)),
            dma((mp, PIECES)),
            dma((seq,)),
            dma((seq,)),
            dma((others,)),
            dma((others,)),
            dma((9,)),
        ],
        compiler_params=pltpu.CompilerParams(
            collective_id=0, has_side_effects=True, vmem_limit_bytes=67043328
        ),
        name="fused_layer",
    )(
        input_lengths.reshape(seq),
        target_home.reshape(seq),
        target_lengths.reshape(seq),
        drop_seed,
        position_bias,
        encoder_hidden[0],
        kv_weight,
        jnp.swapaxes(self_proj[0], 0, 1),
        cross_query[0],
        cotangents[0],
    )
    self_out, cross_out, decoder_grads, hidden_out, position_out = pl.pallas_call(
        deliver,
        out_shape=tuple(shapes),
        in_specs=[vmem] * 5,
        out_specs=(hbm,) * 5,
        scratch_shapes=[dma((5,))],
        compiler_params=pltpu.CompilerParams(vmem_limit_bytes=67043328),
        name="deliver",
    )(*results)
    return (
        cross_out[None],
        self_out[None],
        decoder_grads[None],
        hidden_out[None],
        position_out,
    )


def solution(mesh):
    sizes = (mesh.shape["seq"], mesh.shape["mp"], mesh.shape["dp"])
    placed = (
        P("dp", "seq", None),
        P(None, None, "mp"),
        P("dp", "seq", None, "mp"),
        P("dp", "seq", "mp"),
        P("dp", "seq", None, "mp"),
        P(),
        P("dp", "seq", None),
        P("dp", "seq", None),
        P("dp", "seq", None),
        P(),
    )
    return jax.shard_map(
        functools.partial(body, sizes),
        mesh=mesh,
        in_specs=placed,
        out_specs=(
            P("dp", "seq", "mp"),
            P("dp", "seq", "mp"),
            P("dp", "seq", None, "mp"),
            P("dp", "seq", "mp"),
            P(),
        ),
        check_vma=False,
    )
```

```python
import functools

import jax
import jax.numpy as jnp
from jax import lax
from jax.experimental import pallas as pl
from jax.experimental.pallas import tpu as pltpu
from jax.sharding import PartitionSpec as P

HEAD = 256
TGT_MAX = 8
PIECES = 8
STAGE = 256
GROUP = 4
EARLY = 0

MESH = pl.DeviceIdType.MESH
drop_limit = 6554
keep_factor = 65536.0 / (65536.0 - 6554.0)


def scramble(state):
    state = state ^ ((state >> 16) & 65535)
    state = state * 73244475
    state = state ^ ((state >> 16) & 65535)
    state = state * 73244475
    state = state ^ ((state >> 16) & 65535)
    return state


def keep_table(base, head, query_pos, key_pos):
    state = scramble(base + head)
    state = scramble(state + query_pos)
    state = scramble(state + key_pos)
    return jnp.where((state & 65535) >= drop_limit, keep_factor, 0.0).astype(jnp.float32)


def nt(a, b):
    return lax.dot_general(a, b, (((1,), (1,)), ((), ())), preferred_element_type=jnp.float32)


def nn(a, b):
    return lax.dot_general(a, b, (((1,), (0,)), ((), ())), preferred_element_type=jnp.float32)


def tn(a, b):
    return lax.dot_general(a, b, (((0,), (0,)), ((), ())), preferred_element_type=jnp.float32)


def softmax(scores):
    peak = jnp.max(scores, axis=-1, keepdims=True)
    expo = jnp.exp(scores - peak)
    return expo / jnp.sum(expo, axis=-1, keepdims=True)


def kernel(
    sizes,
    lengths_in,
    homes_in,
    counts_in,
    seed_in,
    bias_in,
    hidden_in,
    weight,
    self_in,
    query_in,
    cotangents_in,
    self_out,
    cross_out,
    decoder_grads,
    hidden_out,
    position_out,
    lengths,
    homes,
    counts,
    seed,
    bias,
    hidden,
    self_proj,
    cross_query,
    cotangents,
    stage,
    w_buf,
    kv_acc,
    kv_buf,
    grad_buf,
    self_grad,
    planes,
    sent,
    got,
    reply,
    got_reply,
    partial_send,
    partial_got,
    pos_seq,
    pos_all,
    w_sem,
    x_send,
    x_recv,
    r_send,
    r_recv,
    h_send,
    h_recv,
    p_send,
    p_recv,
    a_send,
    a_recv,
    in_sem,
):
    seq, mp, dp = sizes
    me = lax.axis_index("seq")
    column = lax.axis_index("mp")
    group = lax.axis_index("dp")
    enc = hidden.shape[0]
    model = hidden.shape[1]
    dec, features = cross_query.shape
    heads = features // HEAD
    factor = HEAD ** (-0.5)
    rows2 = 2 * TGT_MAX
    others = mp * dp
    mine = column * dp + group
    steps = model // STAGE

    def w_copy(n):
        return pltpu.make_async_copy(
            weight.at[pl.ds(n * STAGE, STAGE)], stage.at[n], w_sem.at[n]
        )

    def other_id(k):
        other = lax.rem(mine + k, others)
        return {"mp": other // dp, "dp": lax.rem(other, dp)}

    barrier = pltpu.get_barrier_semaphore()
    for k in range(1, seq):
        pl.semaphore_signal(
            barrier, inc=1, device_id={"seq": lax.rem(me + k, seq)}, device_id_type=MESH
        )

    def greet(k, carry):
        pl.semaphore_signal(barrier, inc=1, device_id=other_id(k), device_id_type=MESH)
        return carry

    lax.fori_loop(1, others, greet, 0)
    incoming = [
        pltpu.make_async_copy(source, target, in_sem.at[i])
        for i, (source, target) in enumerate(
            (
                (counts_in, counts),
                (query_in, cross_query),
                (cotangents_in, cotangents),
                (seed_in, seed),
                (bias_in, bias),
                (self_in, self_proj),
                (hidden_in, hidden),
                (lengths_in, lengths),
                (homes_in, homes),
            )
        )
    ]
    for copy in incoming:
        copy.start()

    def load(n, carry):
        w_copy(n).start()
        return carry

    lax.fori_loop(0, steps, load, 0)
    for copy in incoming[:3]:
        copy.wait()

    def pick(value, which):
        return value.reshape(seq, 2, TGT_MAX, value.shape[1])[:, which].reshape(
            dec, value.shape[1]
        )

    def mix(first, second):
        shape = (seq, 1, TGT_MAX, first.shape[1])
        return jnp.concatenate([first.reshape(shape), second.reshape(shape)], axis=1).reshape(
            2 * dec, first.shape[1]
        )

    def live_rows(width):
        row = lax.broadcasted_iota(jnp.int32, (dec, width), 0)
        count = jnp.zeros((dec, width), jnp.int32)
        for s in range(seq):
            count = jnp.where((row >> 3) == s, counts[s], count)
        return (row & 7) < count

    both_grads = jnp.swapaxes(cotangents[...], 0, 1)
    self_grad[...] = both_grads[0]
    cross_grad = jnp.where(live_rows(features), both_grads[1].astype(jnp.float32), 0.0)
    sent[...] = mix(cross_query[...].astype(jnp.float32), cross_grad).astype(jnp.bfloat16)

    def slot(ref, index):
        return ref.at[pl.ds(pl.multiple_of(index * rows2, rows2), rows2), :]

    def x_copy(k):
        to = lax.rem(me + k, seq)
        return pltpu.make_async_remote_copy(
            src_ref=slot(sent, to),
            dst_ref=slot(got, me),
            send_sem=x_send.at[k],
            recv_sem=x_recv.at[k],
            device_id={"seq": to},
            device_id_type=MESH,
        )

    def r_copy(k):
        to = lax.rem(me + k, seq)
        return pltpu.make_async_remote_copy(
            src_ref=slot(reply, to),
            dst_ref=slot(got_reply, me),
            send_sem=r_send.at[k],
            recv_sem=r_recv.at[k],
            device_id={"seq": to},
            device_id_type=MESH,
        )

    def p_copy(k):
        return pltpu.make_async_remote_copy(
            src_ref=pos_seq.at[me],
            dst_ref=pos_seq.at[me],
            send_sem=p_send.at[k],
            recv_sem=p_recv.at[k],
            device_id={"seq": lax.rem(me + k, seq)},
            device_id_type=MESH,
        )

    def a_copy(k):
        return pltpu.make_async_remote_copy(
            src_ref=pos_all.at[mine],
            dst_ref=pos_all.at[mine],
            send_sem=a_send.at[k],
            recv_sem=a_recv.at[k],
            device_id=other_id(k),
            device_id_type=MESH,
        )

    own_rows = pl.ds(pl.multiple_of(me * rows2, rows2), rows2)
    got[own_rows, :] = sent[own_rows, :]
    for copy in incoming[3:6]:
        copy.wait()

    row = lax.broadcasted_iota(jnp.int32, (dec, dec), 0)
    col = lax.broadcasted_iota(jnp.int32, (dec, dec), 1)
    count = jnp.zeros((dec, dec), jnp.int32)
    for s in range(seq):
        count = jnp.where((row >> 3) == s, counts[s], count)
    distance = row - col
    allowed = ((row >> 3) == (col >> 3)) & (distance >= 0) & ((col & 7) < count)
    live = (row & 7) < count
    base = scramble(seed[0] + 7919 + group * 104729)
    lane = lax.broadcasted_iota(jnp.int32, (TGT_MAX, 128), 1)
    position = jnp.zeros((TGT_MAX, 128), jnp.float32)
    for h in range(heads):
        cols = slice(h * HEAD, (h + 1) * HEAD)
        head = column * heads + h
        q, key, val = self_proj[0, :, cols], self_proj[1, :, cols], self_proj[2, :, cols]
        grad = self_grad[:, cols]
        shift = jnp.zeros((dec, dec), jnp.float32)
        for r in range(TGT_MAX):
            shift = jnp.where(distance == r, bias[r, head], shift)
        probs = softmax(jnp.where(allowed, nt(q, key) * factor + shift, -1e30))
        keep = keep_table(base, head, me * dec + row, me * dec + col)
        weights = jnp.where(live, probs * keep, 0.0).astype(jnp.bfloat16)
        self_out[:, cols] = nn(weights, val).astype(jnp.bfloat16)
        dprobs = nt(grad, val) * keep
        delta = jnp.sum(probs * dprobs, axis=-1, keepdims=True)
        dscores = jnp.where(live, probs * (dprobs - delta), 0.0)
        scaled = (dscores * factor).astype(jnp.bfloat16)
        planes[0, :, cols] = nn(scaled, key).astype(jnp.bfloat16)
        planes[1, :, cols] = tn(scaled, q).astype(jnp.bfloat16)
        planes[2, :, cols] = tn(weights, grad).astype(jnp.bfloat16)
        sums = jnp.concatenate(
            [
                jnp.sum(jnp.where(distance == r, dscores, 0.0), axis=0, keepdims=True)
                for r in range(TGT_MAX)
            ],
            axis=0,
        )
        total = jnp.sum(sums, axis=1, keepdims=True)
        position = jnp.where(lane == head, total, position)
    pos_seq[me] = position

    kv_acc[...] = jnp.zeros_like(kv_acc)
    for copy in incoming[6:]:
        copy.wait()

    wide = GROUP * STAGE

    def arrange(n, carry):
        w_copy(n).wait()
        rows = pl.ds(pl.multiple_of(n * STAGE, STAGE), STAGE)
        w_buf[:, rows, :] = jnp.swapaxes(stage[n], 0, 1)
        return carry

    def project(g, carry):
        lax.fori_loop(g * GROUP, (g + 1) * GROUP, arrange, 0)

        @pl.when(g == EARLY)
        def _():
            pl.semaphore_wait(barrier, seq - 1 + others - 1)
            for k in range(1, seq):
                x_copy(k).start()
            for k in range(1, seq):
                p_copy(k).start()

        rows = pl.ds(pl.multiple_of(g * wide, wide), wide)
        left = hidden[:, rows]
        kv_acc[0] += nn(left, w_buf[0, rows, :])
        kv_acc[1] += nn(left, w_buf[1, rows, :])
        return carry

    lax.fori_loop(0, model // wide, project, 0)
    kv_buf[...] = kv_acc[...].astype(jnp.bfloat16)

    for k in range(1, seq):
        x_copy(k).wait()

    row = lax.broadcasted_iota(jnp.int32, (dec, enc), 0)
    col = lax.broadcasted_iota(jnp.int32, (dec, enc), 1)
    home = jnp.zeros((dec, enc), jnp.int32)
    offset = jnp.int32(0)
    for e in range(seq):
        home = jnp.where(col >= offset, homes[e], home)
        offset = offset + lengths[e]
    allowed = (row >> 3) == home
    query_pos = (row >> 3) * dec + me * TGT_MAX + (row & 7)
    key_pos = me * enc + col
    base = scramble(seed[0] + group * 104729)
    blank = jnp.zeros((dec, enc), jnp.float32)
    for h in range(heads):
        cols = slice(h * HEAD, (h + 1) * HEAD)
        head = column * heads + h
        both = got[:, cols]
        key, val = kv_buf[0, :, cols], kv_buf[1, :, cols]
        probs = softmax(jnp.where(allowed, pick(nt(both, key), 0) * factor, -1e30))
        keep = keep_table(base, head, query_pos, key_pos)
        weights = probs * keep
        dprobs = pick(nt(both, val), 1) * keep
        delta = jnp.sum(probs * dprobs, axis=-1, keepdims=True)
        scaled = probs * (dprobs - delta) * factor
        grad_buf[0, :, cols] = tn(mix(scaled, blank).astype(jnp.bfloat16), both).astype(
            jnp.bfloat16
        )
        grad_buf[1, :, cols] = tn(mix(blank, weights).astype(jnp.bfloat16), both).astype(
            jnp.bfloat16
        )
        reply[:, cols] = mix(
            nn(weights.astype(jnp.bfloat16), val), nn(scaled.astype(jnp.bfloat16), key)
        ).astype(jnp.bfloat16)

    share = model // mp
    piece = share // PIECES

    def product(begin):
        rows = pl.ds(begin, piece)
        total = nt(grad_buf[0], w_buf[0, rows, :]) + nt(grad_buf[1], w_buf[1, rows, :])
        return total.astype(jnp.bfloat16)

    def h_copy(k, i):
        return pltpu.make_async_remote_copy(
            src_ref=partial_send.at[k, i],
            dst_ref=partial_got.at[column, i],
            send_sem=h_send.at[k, i],
            recv_sem=h_recv.at[k, i],
            device_id={"mp": lax.rem(column + k, mp)},
            device_id_type=MESH,
        )

    for k in range(1, seq):
        r_copy(k).start()
    for k in range(1, mp):
        to = lax.rem(column + k, mp)

        def send_piece(i, carry, k=k, to=to):
            partial_send[k, i] = product(pl.multiple_of(to * share + i * piece, piece))
            h_copy(k, i).start()
            return carry

        lax.fori_loop(0, PIECES, send_piece, 0)

    got_reply[own_rows, :] = reply[own_rows, :]
    for k in range(1, seq):
        p_copy(k).wait()
    total = pos_seq[0]
    for s in range(1, seq):
        total = total + pos_seq[s]
    pos_all[mine] = total

    def share_total(k, carry):
        a_copy(k).start()
        return carry

    lax.fori_loop(1, others, share_total, 0)

    def keep_piece(i, carry):
        partial_got[column, i] = product(pl.multiple_of(column * share + i * piece, piece))
        return carry

    lax.fori_loop(0, PIECES, keep_piece, 0)
    for k in range(1, seq):
        r_copy(k).wait()
    back = got_reply[...].astype(jnp.float32)
    cross_out[...] = jnp.where(live_rows(features), pick(back, 0), 0.0).astype(jnp.bfloat16)
    planes[3] = pick(back, 1).astype(jnp.bfloat16)
    decoder_grads[...] = jnp.swapaxes(planes[...], 0, 1)

    def take_total(k, carry):
        a_copy(k).wait()
        return carry

    lax.fori_loop(1, others, take_total, 0)
    total = pos_all[0]
    for m in range(1, others):
        total = total + pos_all[m]
    position_out[...] = total[:, : position_out.shape[1]]

    for i in range(PIECES):
        for k in range(1, mp):
            h_copy(k, i).wait()
        total = partial_got[0, i].astype(jnp.float32)
        for m in range(1, mp):
            total = total + partial_got[m, i].astype(jnp.float32)
        hidden_out[:, i * piece : (i + 1) * piece] = total.astype(jnp.bfloat16)


def deliver(*refs):
    taken, given, done = refs[:5], refs[5:10], refs[10]
    copies = [pltpu.make_async_copy(taken[i], given[i], done.at[i]) for i in range(5)]
    for copy in copies:
        copy.start()
    for copy in copies:
        copy.wait()


def body(
    sizes,
    encoder_hidden,
    kv_weight,
    self_proj,
    cross_query,
    cotangents,
    position_bias,
    input_lengths,
    target_home,
    target_lengths,
    drop_seed,
):
    seq, mp, dp = sizes
    enc, model = encoder_hidden.shape[1:]
    dec, features = cross_query.shape[1:]
    share = model // mp
    others = mp * dp
    vmem = pl.BlockSpec(memory_space=pltpu.VMEM)
    far = pl.BlockSpec(memory_space=pltpu.HBM)
    hbm = pl.BlockSpec(memory_space=pl.ANY)
    half = jnp.bfloat16
    dma = pltpu.SemaphoreType.DMA
    shapes = [
        jax.ShapeDtypeStruct((dec, features), half),
        jax.ShapeDtypeStruct((dec, features), half),
        jax.ShapeDtypeStruct((dec, 4, features), half),
        jax.ShapeDtypeStruct((enc, share), half),
        jax.ShapeDtypeStruct(position_bias.shape, jnp.float32),
    ]
    results = pl.pallas_call(
        functools.partial(kernel, sizes),
        out_shape=tuple(shapes),
        in_specs=[far] * 10,
        out_specs=(vmem,) * 5,
        scratch_shapes=[
            pltpu.SMEM((seq,), jnp.int32),
            pltpu.SMEM((seq,), jnp.int32),
            pltpu.SMEM((seq,), jnp.int32),
            pltpu.SMEM((1,), jnp.int32),
            pltpu.SMEM(position_bias.shape, jnp.float32),
            pltpu.VMEM((enc, model), half),
            pltpu.VMEM((3, dec, features), half),
            pltpu.VMEM((dec, features), half),
            pltpu.VMEM((dec, 2, features), half),
            pltpu.VMEM((model // STAGE, STAGE, 2, features), half),
            pltpu.VMEM((2, model, features), half),
            pltpu.VMEM((2, enc, features), jnp.float32),
            pltpu.VMEM((2, enc, features), half),
            pltpu.VMEM((2, enc, features), half),
            pltpu.VMEM((dec, features), half),
            pltpu.VMEM((4, dec, features), half),
            pltpu.VMEM((2 * dec, features), half),
            pltpu.VMEM((2 * dec, features), half),
            pltpu.VMEM((2 * dec, features), half),
            pltpu.VMEM((2 * dec, features), half),
            pltpu.VMEM((mp, PIECES, enc, share // PIECES), half),
            pltpu.VMEM((mp, PIECES, enc, share // PIECES), half),
            pltpu.VMEM((seq, TGT_MAX, 128), jnp.float32),
            pltpu.VMEM((others, TGT_MAX, 128), jnp.float32),
            dma((model // STAGE,)),
            dma((seq,)),
            dma((seq,)),
            dma((seq,)),
            dma((seq,)),
            dma((mp, PIECES)),
            dma((mp, PIECES)),
            dma((seq,)),
            dma((seq,)),
            dma((others,)),
            dma((others,)),
            dma((9,)),
        ],
        compiler_params=pltpu.CompilerParams(
            collective_id=0, has_side_effects=True, vmem_limit_bytes=67043328
        ),
        name="fused_layer",
    )(
        input_lengths.reshape(seq),
        target_home.reshape(seq),
        target_lengths.reshape(seq),
        drop_seed,
        position_bias,
        encoder_hidden[0],
        kv_weight,
        jnp.swapaxes(self_proj[0], 0, 1),
        cross_query[0],
        cotangents[0],
    )
    self_out, cross_out, decoder_grads, hidden_out, position_out = pl.pallas_call(
        deliver,
        out_shape=tuple(shapes),
        in_specs=[vmem] * 5,
        out_specs=(hbm,) * 5,
        scratch_shapes=[dma((5,))],
        compiler_params=pltpu.CompilerParams(vmem_limit_bytes=67043328),
        name="deliver",
    )(*results)
    return (
        cross_out[None],
        self_out[None],
        decoder_grads[None],
        hidden_out[None],
        position_out,
    )


def solution(mesh):
    sizes = (mesh.shape["seq"], mesh.shape["mp"], mesh.shape["dp"])
    placed = (
        P("dp", "seq", None),
        P(None, None, "mp"),
        P("dp", "seq", None, "mp"),
        P("dp", "seq", "mp"),
        P("dp", "seq", None, "mp"),
        P(),
        P("dp", "seq", None),
        P("dp", "seq", None),
        P("dp", "seq", None),
        P(),
    )
    return jax.shard_map(
        functools.partial(body, sizes),
        mesh=mesh,
        in_specs=placed,
        out_specs=(
            P("dp", "seq", "mp"),
            P("dp", "seq", "mp"),
            P("dp", "seq", None, "mp"),
            P("dp", "seq", "mp"),
            P(),
        ),
        check_vma=False,
    )
```

```python
import functools

import jax
import jax.numpy as jnp
from jax import lax
from jax.experimental import pallas as pl
from jax.experimental.pallas import tpu as pltpu
from jax.sharding import PartitionSpec as P

HEAD = 256
TGT_MAX = 8
PIECES = 8
STAGE = 256
GROUP = 4
EARLY = 0

MESH = pl.DeviceIdType.MESH
drop_limit = 6554
keep_factor = 65536.0 / (65536.0 - 6554.0)


def scramble(state):
    state = state ^ ((state >> 16) & 65535)
    state = state * 73244475
    state = state ^ ((state >> 16) & 65535)
    state = state * 73244475
    state = state ^ ((state >> 16) & 65535)
    return state


def keep_table(base, head, query_pos, key_pos):
    state = scramble(base + head)
    state = scramble(state + query_pos)
    state = scramble(state + key_pos)
    return jnp.where((state & 65535) >= drop_limit, keep_factor, 0.0).astype(jnp.float32)


def nt(a, b):
    return lax.dot_general(a, b, (((1,), (1,)), ((), ())), preferred_element_type=jnp.float32)


def nn(a, b):
    return lax.dot_general(a, b, (((1,), (0,)), ((), ())), preferred_element_type=jnp.float32)


def tn(a, b):
    return lax.dot_general(a, b, (((0,), (0,)), ((), ())), preferred_element_type=jnp.float32)


def softmax(scores):
    peak = jnp.max(scores, axis=-1, keepdims=True)
    expo = jnp.exp(scores - peak)
    return expo / jnp.sum(expo, axis=-1, keepdims=True)


def kernel(
    sizes,
    lengths_in,
    homes_in,
    counts_in,
    seed_in,
    bias_in,
    hidden_in,
    weight,
    self_in,
    query_in,
    cotangents_in,
    self_out,
    cross_out,
    decoder_grads,
    hidden_out,
    position_out,
    lengths,
    homes,
    counts,
    seed,
    bias,
    hidden,
    self_proj,
    cross_query,
    cotangents,
    stage,
    w_buf,
    kv_acc,
    kv_buf,
    grad_buf,
    self_grad,
    planes,
    sent,
    got,
    reply,
    got_reply,
    partial_send,
    partial_got,
    pos_seq,
    pos_all,
    w_sem,
    x_send,
    x_recv,
    r_send,
    r_recv,
    h_send,
    h_recv,
    p_send,
    p_recv,
    a_send,
    a_recv,
    in_sem,
    keeps,
):
    seq, mp, dp = sizes
    me = lax.axis_index("seq")
    column = lax.axis_index("mp")
    group = lax.axis_index("dp")
    enc = hidden.shape[0]
    model = hidden.shape[1]
    dec, features = cross_query.shape
    heads = features // HEAD
    factor = HEAD ** (-0.5)
    rows2 = 2 * TGT_MAX
    others = mp * dp
    mine = column * dp + group
    steps = model // STAGE

    def w_copy(n):
        return pltpu.make_async_copy(
            weight.at[pl.ds(n * STAGE, STAGE)], stage.at[n], w_sem.at[n]
        )

    def other_id(k):
        other = lax.rem(mine + k, others)
        return {"mp": other // dp, "dp": lax.rem(other, dp)}

    barrier = pltpu.get_barrier_semaphore()
    for k in range(1, seq):
        pl.semaphore_signal(
            barrier, inc=1, device_id={"seq": lax.rem(me + k, seq)}, device_id_type=MESH
        )

    def greet(k, carry):
        pl.semaphore_signal(barrier, inc=1, device_id=other_id(k), device_id_type=MESH)
        return carry

    lax.fori_loop(1, others, greet, 0)
    incoming = [
        pltpu.make_async_copy(source, target, in_sem.at[i])
        for i, (source, target) in enumerate(
            (
                (counts_in, counts),
                (query_in, cross_query),
                (cotangents_in, cotangents),
                (seed_in, seed),
                (bias_in, bias),
                (self_in, self_proj),
                (hidden_in, hidden),
                (lengths_in, lengths),
                (homes_in, homes),
            )
        )
    ]
    for copy in incoming:
        copy.start()

    def load(n, carry):
        w_copy(n).start()
        return carry

    lax.fori_loop(0, steps, load, 0)
    for copy in incoming[:3]:
        copy.wait()

    def pick(value, which):
        return value.reshape(seq, 2, TGT_MAX, value.shape[1])[:, which].reshape(
            dec, value.shape[1]
        )

    def mix(first, second):
        shape = (seq, 1, TGT_MAX, first.shape[1])
        return jnp.concatenate([first.reshape(shape), second.reshape(shape)], axis=1).reshape(
            2 * dec, first.shape[1]
        )

    def live_rows(width):
        row = lax.broadcasted_iota(jnp.int32, (dec, width), 0)
        count = jnp.zeros((dec, width), jnp.int32)
        for s in range(seq):
            count = jnp.where((row >> 3) == s, counts[s], count)
        return (row & 7) < count

    both_grads = jnp.swapaxes(cotangents[...], 0, 1)
    self_grad[...] = both_grads[0]
    cross_grad = jnp.where(live_rows(features), both_grads[1].astype(jnp.float32), 0.0)
    sent[...] = mix(cross_query[...].astype(jnp.float32), cross_grad).astype(jnp.bfloat16)

    def slot(ref, index):
        return ref.at[pl.ds(pl.multiple_of(index * rows2, rows2), rows2), :]

    def x_copy(k):
        to = lax.rem(me + k, seq)
        return pltpu.make_async_remote_copy(
            src_ref=slot(sent, to),
            dst_ref=slot(got, me),
            send_sem=x_send.at[k],
            recv_sem=x_recv.at[k],
            device_id={"seq": to},
            device_id_type=MESH,
        )

    def r_copy(k):
        to = lax.rem(me + k, seq)
        return pltpu.make_async_remote_copy(
            src_ref=slot(reply, to),
            dst_ref=slot(got_reply, me),
            send_sem=r_send.at[k],
            recv_sem=r_recv.at[k],
            device_id={"seq": to},
            device_id_type=MESH,
        )

    def p_copy(k):
        return pltpu.make_async_remote_copy(
            src_ref=pos_seq.at[me],
            dst_ref=pos_seq.at[me],
            send_sem=p_send.at[k],
            recv_sem=p_recv.at[k],
            device_id={"seq": lax.rem(me + k, seq)},
            device_id_type=MESH,
        )

    def a_copy(k):
        return pltpu.make_async_remote_copy(
            src_ref=pos_all.at[mine],
            dst_ref=pos_all.at[mine],
            send_sem=a_send.at[k],
            recv_sem=a_recv.at[k],
            device_id=other_id(k),
            device_id_type=MESH,
        )

    own_rows = pl.ds(pl.multiple_of(me * rows2, rows2), rows2)
    got[own_rows, :] = sent[own_rows, :]
    for copy in incoming[3:6]:
        copy.wait()

    row = lax.broadcasted_iota(jnp.int32, (dec, dec), 0)
    col = lax.broadcasted_iota(jnp.int32, (dec, dec), 1)
    count = jnp.zeros((dec, dec), jnp.int32)
    for s in range(seq):
        count = jnp.where((row >> 3) == s, counts[s], count)
    distance = row - col
    allowed = ((row >> 3) == (col >> 3)) & (distance >= 0) & ((col & 7) < count)
    live = (row & 7) < count
    base = scramble(seed[0] + 7919 + group * 104729)
    lane = lax.broadcasted_iota(jnp.int32, (TGT_MAX, 128), 1)
    position = jnp.zeros((TGT_MAX, 128), jnp.float32)
    for h in range(heads):
        cols = slice(h * HEAD, (h + 1) * HEAD)
        head = column * heads + h
        q, key, val = self_proj[0, :, cols], self_proj[1, :, cols], self_proj[2, :, cols]
        grad = self_grad[:, cols]
        shift = jnp.zeros((dec, dec), jnp.float32)
        for r in range(TGT_MAX):
            shift = jnp.where(distance == r, bias[r, head], shift)
        probs = softmax(jnp.where(allowed, nt(q, key) * factor + shift, -1e30))
        keep = keep_table(base, head, me * dec + row, me * dec + col)
        weights = jnp.where(live, probs * keep, 0.0).astype(jnp.bfloat16)
        self_out[:, cols] = nn(weights, val).astype(jnp.bfloat16)
        dprobs = nt(grad, val) * keep
        delta = jnp.sum(probs * dprobs, axis=-1, keepdims=True)
        dscores = jnp.where(live, probs * (dprobs - delta), 0.0)
        scaled = (dscores * factor).astype(jnp.bfloat16)
        planes[0, :, cols] = nn(scaled, key).astype(jnp.bfloat16)
        planes[1, :, cols] = tn(scaled, q).astype(jnp.bfloat16)
        planes[2, :, cols] = tn(weights, grad).astype(jnp.bfloat16)
        sums = jnp.concatenate(
            [
                jnp.sum(jnp.where(distance == r, dscores, 0.0), axis=0, keepdims=True)
                for r in range(TGT_MAX)
            ],
            axis=0,
        )
        total = jnp.sum(sums, axis=1, keepdims=True)
        position = jnp.where(lane == head, total, position)
    pos_seq[me] = position

    kv_acc[...] = jnp.zeros_like(kv_acc)
    for copy in incoming[6:]:
        copy.wait()

    wide = GROUP * STAGE

    def arrange(n, carry):
        w_copy(n).wait()
        rows = pl.ds(pl.multiple_of(n * STAGE, STAGE), STAGE)
        w_buf[:, rows, :] = jnp.swapaxes(stage[n], 0, 1)
        return carry

    def project(g, carry):
        lax.fori_loop(g * GROUP, (g + 1) * GROUP, arrange, 0)

        @pl.when(g == EARLY)
        def _():
            pl.semaphore_wait(barrier, seq - 1 + others - 1)
            for k in range(1, seq):
                x_copy(k).start()

        rows = pl.ds(pl.multiple_of(g * wide, wide), wide)
        left = hidden[:, rows]
        kv_acc[0] += nn(left, w_buf[0, rows, :])
        kv_acc[1] += nn(left, w_buf[1, rows, :])
        return carry

    lax.fori_loop(0, model // wide, project, 0)
    kv_buf[...] = kv_acc[...].astype(jnp.bfloat16)

    row = lax.broadcasted_iota(jnp.int32, (dec, enc), 0)
    col = lax.broadcasted_iota(jnp.int32, (dec, enc), 1)
    home = jnp.zeros((dec, enc), jnp.int32)
    offset = jnp.int32(0)
    for e in range(seq):
        home = jnp.where(col >= offset, homes[e], home)
        offset = offset + lengths[e]
    allowed = (row >> 3) == home
    query_pos = (row >> 3) * dec + me * TGT_MAX + (row & 7)
    key_pos = me * enc + col
    base = scramble(seed[0] + group * 104729)
    for h in range(heads):
        keeps[h] = keep_table(base, column * heads + h, query_pos, key_pos)
    for k in range(1, seq):
        x_copy(k).wait()
    for k in range(1, seq):
        p_copy(k).start()

    blank = jnp.zeros((dec, enc), jnp.float32)
    for h in range(heads):
        cols = slice(h * HEAD, (h + 1) * HEAD)
        head = column * heads + h
        both = got[:, cols]
        key, val = kv_buf[0, :, cols], kv_buf[1, :, cols]
        probs = softmax(jnp.where(allowed, pick(nt(both, key), 0) * factor, -1e30))
        keep = keeps[h]
        weights = probs * keep
        dprobs = pick(nt(both, val), 1) * keep
        delta = jnp.sum(probs * dprobs, axis=-1, keepdims=True)
        scaled = probs * (dprobs - delta) * factor
        grad_buf[0, :, cols] = tn(mix(scaled, blank).astype(jnp.bfloat16), both).astype(
            jnp.bfloat16
        )
        grad_buf[1, :, cols] = tn(mix(blank, weights).astype(jnp.bfloat16), both).astype(
            jnp.bfloat16
        )
        reply[:, cols] = mix(
            nn(weights.astype(jnp.bfloat16), val), nn(scaled.astype(jnp.bfloat16), key)
        ).astype(jnp.bfloat16)

    share = model // mp
    piece = share // PIECES

    def product(begin):
        rows = pl.ds(begin, piece)
        total = nt(grad_buf[0], w_buf[0, rows, :]) + nt(grad_buf[1], w_buf[1, rows, :])
        return total.astype(jnp.bfloat16)

    def h_copy(k, i):
        return pltpu.make_async_remote_copy(
            src_ref=partial_send.at[k, i],
            dst_ref=partial_got.at[column, i],
            send_sem=h_send.at[k, i],
            recv_sem=h_recv.at[k, i],
            device_id={"mp": lax.rem(column + k, mp)},
            device_id_type=MESH,
        )

    for k in range(1, mp):
        to = lax.rem(column + k, mp)

        def send_piece(i, carry, k=k, to=to):
            partial_send[k, i] = product(pl.multiple_of(to * share + i * piece, piece))
            h_copy(k, i).start()
            return carry

        lax.fori_loop(0, 1, send_piece, 0)
        if k == 1:
            for q in range(1, seq):
                r_copy(q).start()
        lax.fori_loop(1, PIECES, send_piece, 0)

    got_reply[own_rows, :] = reply[own_rows, :]
    for k in range(1, seq):
        p_copy(k).wait()
    total = pos_seq[0]
    for s in range(1, seq):
        total = total + pos_seq[s]
    pos_all[mine] = total

    def share_total(k, carry):
        a_copy(k).start()
        return carry

    lax.fori_loop(1, others, share_total, 0)

    def keep_piece(i, carry):
        partial_got[column, i] = product(pl.multiple_of(column * share + i * piece, piece))
        return carry

    lax.fori_loop(0, PIECES, keep_piece, 0)
    for k in range(1, seq):
        r_copy(k).wait()
    back = got_reply[...].astype(jnp.float32)
    cross_out[...] = jnp.where(live_rows(features), pick(back, 0), 0.0).astype(jnp.bfloat16)
    planes[3] = pick(back, 1).astype(jnp.bfloat16)
    decoder_grads[...] = jnp.swapaxes(planes[...], 0, 1)

    def take_total(k, carry):
        a_copy(k).wait()
        return carry

    lax.fori_loop(1, others, take_total, 0)
    total = pos_all[0]
    for m in range(1, others):
        total = total + pos_all[m]
    position_out[...] = total[:, : position_out.shape[1]]

    for i in range(PIECES):
        for k in range(1, mp):
            h_copy(k, i).wait()
        total = partial_got[0, i].astype(jnp.float32)
        for m in range(1, mp):
            total = total + partial_got[m, i].astype(jnp.float32)
        hidden_out[:, i * piece : (i + 1) * piece] = total.astype(jnp.bfloat16)


def deliver(*refs):
    taken, given, done = refs[:5], refs[5:10], refs[10]
    copies = [pltpu.make_async_copy(taken[i], given[i], done.at[i]) for i in range(5)]
    for copy in copies:
        copy.start()
    for copy in copies:
        copy.wait()


def body(
    sizes,
    encoder_hidden,
    kv_weight,
    self_proj,
    cross_query,
    cotangents,
    position_bias,
    input_lengths,
    target_home,
    target_lengths,
    drop_seed,
):
    seq, mp, dp = sizes
    enc, model = encoder_hidden.shape[1:]
    dec, features = cross_query.shape[1:]
    share = model // mp
    others = mp * dp
    vmem = pl.BlockSpec(memory_space=pltpu.VMEM)
    far = pl.BlockSpec(memory_space=pltpu.HBM)
    hbm = pl.BlockSpec(memory_space=pl.ANY)
    half = jnp.bfloat16
    dma = pltpu.SemaphoreType.DMA
    shapes = [
        jax.ShapeDtypeStruct((dec, features), half),
        jax.ShapeDtypeStruct((dec, features), half),
        jax.ShapeDtypeStruct((dec, 4, features), half),
        jax.ShapeDtypeStruct((enc, share), half),
        jax.ShapeDtypeStruct(position_bias.shape, jnp.float32),
    ]
    results = pl.pallas_call(
        functools.partial(kernel, sizes),
        out_shape=tuple(shapes),
        in_specs=[far] * 10,
        out_specs=(vmem,) * 5,
        scratch_shapes=[
            pltpu.SMEM((seq,), jnp.int32),
            pltpu.SMEM((seq,), jnp.int32),
            pltpu.SMEM((seq,), jnp.int32),
            pltpu.SMEM((1,), jnp.int32),
            pltpu.SMEM(position_bias.shape, jnp.float32),
            pltpu.VMEM((enc, model), half),
            pltpu.VMEM((3, dec, features), half),
            pltpu.VMEM((dec, features), half),
            pltpu.VMEM((dec, 2, features), half),
            pltpu.VMEM((model // STAGE, STAGE, 2, features), half),
            pltpu.VMEM((2, model, features), half),
            pltpu.VMEM((2, enc, features), jnp.float32),
            pltpu.VMEM((2, enc, features), half),
            pltpu.VMEM((2, enc, features), half),
            pltpu.VMEM((dec, features), half),
            pltpu.VMEM((4, dec, features), half),
            pltpu.VMEM((2 * dec, features), half),
            pltpu.VMEM((2 * dec, features), half),
            pltpu.VMEM((2 * dec, features), half),
            pltpu.VMEM((2 * dec, features), half),
            pltpu.VMEM((mp, PIECES, enc, share // PIECES), half),
            pltpu.VMEM((mp, PIECES, enc, share // PIECES), half),
            pltpu.VMEM((seq, TGT_MAX, 128), jnp.float32),
            pltpu.VMEM((others, TGT_MAX, 128), jnp.float32),
            dma((model // STAGE,)),
            dma((seq,)),
            dma((seq,)),
            dma((seq,)),
            dma((seq,)),
            dma((mp, PIECES)),
            dma((mp, PIECES)),
            dma((seq,)),
            dma((seq,)),
            dma((others,)),
            dma((others,)),
            dma((9,)),
            pltpu.VMEM((features // HEAD, dec, enc), jnp.float32),
        ],
        compiler_params=pltpu.CompilerParams(
            collective_id=0, has_side_effects=True, vmem_limit_bytes=67043328
        ),
        name="fused_layer",
    )(
        input_lengths.reshape(seq),
        target_home.reshape(seq),
        target_lengths.reshape(seq),
        drop_seed,
        position_bias,
        encoder_hidden[0],
        kv_weight,
        jnp.swapaxes(self_proj[0], 0, 1),
        cross_query[0],
        cotangents[0],
    )
    self_out, cross_out, decoder_grads, hidden_out, position_out = pl.pallas_call(
        deliver,
        out_shape=tuple(shapes),
        in_specs=[vmem] * 5,
        out_specs=(hbm,) * 5,
        scratch_shapes=[dma((5,))],
        compiler_params=pltpu.CompilerParams(vmem_limit_bytes=67043328),
        name="deliver",
    )(*results)
    return (
        cross_out[None],
        self_out[None],
        decoder_grads[None],
        hidden_out[None],
        position_out,
    )


def solution(mesh):
    sizes = (mesh.shape["seq"], mesh.shape["mp"], mesh.shape["dp"])
    placed = (
        P("dp", "seq", None),
        P(None, None, "mp"),
        P("dp", "seq", None, "mp"),
        P("dp", "seq", "mp"),
        P("dp", "seq", None, "mp"),
        P(),
        P("dp", "seq", None),
        P("dp", "seq", None),
        P("dp", "seq", None),
        P(),
    )
    return jax.shard_map(
        functools.partial(body, sizes),
        mesh=mesh,
        in_specs=placed,
        out_specs=(
            P("dp", "seq", "mp"),
            P("dp", "seq", "mp"),
            P("dp", "seq", None, "mp"),
            P("dp", "seq", "mp"),
            P(),
        ),
        check_vma=False,
    )
```
